128 devices in a mesh: section: 8 (over x_lo, z), tp: 16 (over y, x_hi, core).
Axes of the slice: x: 4 (x_hi: 2, x_lo: 2; x = x_hi * 2 + x_lo), y: 4, z: 4, core: 2. Of those that a mesh axis runs over, the one named last changes fastest.
Arguments:
- stash: bfloat16 [8, 4, 192, 1024], P('section', None, 'tp'), may hold values from -6 to 6
- w_in: bfloat16 [8, 1024, 65536], P('section', None, 'tp'), may hold values from -0.1875 to 0.1875
- w_out: bfloat16 [8, 65536, 1024], P('section', 'tp'), may hold values from -0.0234375 to 0.0234375
- gain: float32 [8, 1024], P('section'), may hold values from 0.1 to 1.9
- plan: int32 [3, 8], replicated, may hold values from 0 to 3
- arriving: bfloat16 [8, 192, 1024], P('section', 'tp'), may hold values from -6 to 6
- fresh: bfloat16 [2, 192, 1024], P(None, 'tp'), may hold values from -6 to 6
Outputs:
- input_grads: bfloat16 [3, 8, 192, 1024], P(None, 'section', 'tp')
The draws below stay inside these ranges and needn't reach their ends.
All inputs are finite; a program needn't handle non-finite values.
Results may differ from the reference program's by a relative error of at most 0.0085.
Values may be sent and summed in bfloat16 or wider, within the bound.
A program may use at most 64 MiB of HBM per device.

```python
import jax
import jax.numpy as jnp
from jax import lax

D = 1024
FF = 65536
TOK = 192
SLOTS = 4
TICKS = 3
SECTIONS = 8


def touch_ends(values, stream_key, low, largest):
    longest = values.shape.index(max(values.shape))
    spots = []
    for shift in (0, 1):
        where = [jax.random.randint(jax.random.fold_in(stream_key, axis), (), 0, length) for axis, length in enumerate(values.shape)]
        where[longest] = (where[longest] + shift) % values.shape[longest]
        spots.append(tuple(where))
    return values.at[spots[0]].set(low).at[spots[1]].set(largest)


def level_of(stream_key, shape, cuts, low, top_value):
    factor_of = 1.0
    for dim, parts in cuts:
        steps = jax.random.uniform(jax.random.fold_in(jax.random.fold_in(stream_key, 6), dim), (parts,), jnp.float32, low / len(cuts), top_value / len(cuts))
        factor_of = factor_of * jnp.repeat(jnp.exp(steps), shape[dim] // parts).reshape((-1,) + (1,) * (len(shape) - 1 - dim))
    return factor_of


def gaussian(rng, extent, deviation, most, shards=(), dtype=jnp.bfloat16):
    array = jax.random.normal(rng, extent, jnp.float32) * deviation
    if len(shards) > 0:
        array = level_of(rng, extent, shards, -0.22, 0.18) * array
    return jnp.clip(array, min=-most, max=most).astype(dtype)


def setup_inputs(seed: int = 0) -> dict:
    key_of = jax.random.split(jax.random.key(seed), 8)
    return {
        "stash": gaussian(key_of[0], (SECTIONS, SLOTS, TOK, D), 1.0, 6.0, ((0, 8), (2, 16))),
        "w_in": gaussian(key_of[1], (SECTIONS, D, FF), D ** -0.5, 0.1875, ((0, 8), (2, 16))),
        "w_out": gaussian(key_of[2], (SECTIONS, FF, D), FF ** -0.5, 0.0234375, ((0, 8), (1, 16))),
        "gain": jnp.clip(1.0 + 0.18 * jax.random.normal(key_of[3], (SECTIONS, D), jnp.float32), 0.1, 1.9),
        "plan": touch_ends(jax.random.randint(key_of[4], (TICKS, SECTIONS), 0, SLOTS), jax.random.fold_in(key_of[4], 1), 0, SLOTS - 1).astype(jnp.int32),
        "arriving": gaussian(key_of[5], (SECTIONS, TOK, D), 1.0, 6.0, ((0, 8), (1, 16))),
        "fresh": gaussian(key_of[6], (TICKS - 1, TOK, D), 1.0, 6.0, ((1, 16),)),
    }


epsilon = 1e-06

def norm_parts(x_rows):
    values = x_rows.astype(jnp.float32)
    inverse_rms = lax.rsqrt(lax.optimization_barrier(jnp.mean(values * values, axis=-1, keepdims=True)) + epsilon)
    return (inverse_rms, values * inverse_rms)

def norm_back(normed_grad, incoming, inverse_rms, normed, gain_row):
    scaled = normed_grad * gain_row
    inner = lax.optimization_barrier(jnp.mean(scaled * normed, axis=-1, keepdims=True))
    return (incoming.astype(jnp.float32) + inverse_rms * (scaled - normed * inner)).astype(jnp.bfloat16)

def section_grad(x_rows, incoming, weight_in, weight_out, gain_row):
    inverse_rms, normed = norm_parts(x_rows)
    inputs = (normed * gain_row).astype(jnp.bfloat16)
    preact = jnp.dot(inputs, weight_in, preferred_element_type=jnp.float32)
    hidden_back = jnp.dot(incoming, weight_out.T, preferred_element_type=jnp.float32)
    hidden_grad = (hidden_back * (2.0 * jnp.maximum(preact, 0.0))).astype(jnp.bfloat16)
    normed_grad = jnp.dot(hidden_grad, weight_in.T, preferred_element_type=jnp.float32)
    return norm_back(normed_grad, incoming, inverse_rms, normed, gain_row)

def reference(stash, w_in, w_out, gain, plan, arriving, fresh):
    results = []
    incoming_all = arriving
    for tick in range(TICKS):
        section_grads = []
        for section_index in range(SECTIONS):
            keeper = (section_index + SECTIONS // 2) % SECTIONS
            x_rows = stash[keeper, plan[tick, section_index]]
            section_grads.append(section_grad(x_rows, incoming_all[section_index], w_in[section_index], w_out[section_index], gain[section_index]))
        section_grads = jnp.stack(section_grads)
        results.append(section_grads)
        if tick + 1 < TICKS:
            incoming_all = jnp.concatenate([section_grads[1:], fresh[tick][None]], axis=0)
    return jnp.stack(results)
```

```python
import functools

import jax
import jax.numpy as jnp
from jax import lax
from jax.experimental import pallas as pl
from jax.experimental.pallas import tpu as pltpu
from jax.sharding import PartitionSpec as P

epsilon = 1e-06
contract_last = (((1,), (1,)), ((), ()))
bf16, f32 = jnp.bfloat16, jnp.float32
PAD = 16
IN_TILE = 512
OUT_TILE = 256


def norm_parts(x_rows):
    values = x_rows.astype(f32)
    inverse_rms = lax.rsqrt(jnp.mean(values * values, axis=-1, keepdims=True) + epsilon)
    return inverse_rms, values * inverse_rms


def window_kernel(
    sections, tps, ticks,
    plan, stash, w_in, w_out, gain, arriving, fresh, out,
    wi, wo, stash_v, own, picks, x_all, inc_all, factor, hidden, acc, part, core_in, half, rs_in, out_v, up,
    load_sem, x_send, x_recv, xf_send, xf_recv, ag_send, ag_recv, agf_send, agf_recv,
    core_send, core_recv, rs_send, rs_recv, up_send, up_recv,
):
    section = lax.axis_index("section")
    me = lax.axis_index("tp")
    core = lax.rem(me, 2)
    place = me // 2
    places = tps // 2
    rows = stash.shape[1]
    width = stash.shape[2]
    units = wo.shape[0]
    mirror = lax.rem(section + sections // 2, sections)
    above = lax.rem(section + 1, sections)
    below = lax.rem(section + sections - 1, sections)
    mine = pl.multiple_of(core * places, places)
    theirs = pl.multiple_of((1 - core) * places, places)
    partner = me + 1 - 2 * core

    def remote(src, dst, send, recv, to_section, to_tp):
        return pltpu.make_async_remote_copy(
            src_ref=src, dst_ref=dst, send_sem=send, recv_sem=recv,
            device_id={"section": to_section, "tp": to_tp}, device_id_type=pl.DeviceIdType.MESH)

    def wait_for(ref, sem):
        pltpu.make_async_copy(ref, ref, sem).wait()

    def other_place(k):
        return lax.bitwise_xor(place, k)

    loads = [
        pltpu.make_async_copy(stash, stash_v, load_sem.at[0]),
        pltpu.make_async_copy(w_in, wi, load_sem.at[1]),
        pltpu.make_async_copy(w_out, wo, load_sem.at[2]),
    ]
    for load in loads:
        load.start()

    barrier = pltpu.get_barrier_semaphore()

    def greet(to_section, to_tp):
        pl.semaphore_signal(barrier, inc=1, device_id={"section": to_section, "tp": to_tp},
                            device_id_type=pl.DeviceIdType.MESH)

    greet(section, partner)
    for k in range(1, places):
        greet(section, other_place(k) * 2 + core)
    for k in range(places):
        greet(mirror, other_place(k) * 2 + core)
    greet(above, me)
    greet(below, me)

    own[...] = jnp.zeros_like(own)
    picks[...] = jnp.zeros_like(picks)
    own[0, 0:rows] = arriving[...]
    loads[0].wait()
    for t in range(ticks):
        picks[t, 0:rows] = stash_v[plan[t, mirror]]
    pl.semaphore_wait(barrier, 2 * places + 2)

    def send_x(t):
        for k in range(places):
            remote(picks.at[t], x_all.at[t, mine + place], x_send.at[t], x_recv.at[t],
                   mirror, other_place(k) * 2 + core).start()

    def send_incoming(t, src):
        pltpu.make_async_copy(src, inc_all.at[t, mine + place], ag_recv.at[t]).start()
        for k in (2, 6, 4, 1, 3, 7, 5):
            remote(src, inc_all.at[t, mine + place], ag_send.at[t], ag_recv.at[t],
                   section, other_place(k) * 2 + core).start()

    def forward(buf, t, recv, f_send, f_recv):
        block = buf.at[t, pl.ds(mine, places)]
        wait_for(block, recv.at[t])
        remote(block, block, f_send.at[t], f_recv.at[t], section, partner).start()

    def forwarded(buf, t, f_send, f_recv):
        wait_for(buf.at[t, pl.ds(mine, places)], f_send.at[t])
        wait_for(buf.at[t, pl.ds(theirs, places)], f_recv.at[t])

    gain_row = gain[...]

    def preact(t):
        forwarded(x_all, t, xf_send, xf_recv)
        _, normed = norm_parts(x_all[t].reshape(tps * PAD, width))
        inputs = (normed * gain_row).astype(bf16)

        def step(n, carry):
            cols = pl.ds(pl.multiple_of(n * IN_TILE, IN_TILE), IN_TILE)
            pre = jnp.dot(inputs, wi[:, cols], preferred_element_type=f32)
            factor[t, :, cols] = 2.0 * jnp.maximum(pre, 0.0)
            return carry

        lax.fori_loop(0, units // IN_TILE, step, 0)

    send_x(0)
    send_incoming(0, own.at[0])
    for t in range(1, ticks):
        send_x(t)
    for t in range(ticks - 1):
        own[t + 1, 0:rows] = fresh[t]
    loads[1].wait()
    loads[2].wait()
    forward(x_all, 0, x_recv, xf_send, xf_recv)
    forward(inc_all, 0, ag_recv, agf_send, agf_recv)
    preact(0)

    for t in range(ticks):
        forwarded(inc_all, t, agf_send, agf_recv)
        incoming = inc_all[t].reshape(tps * PAD, width)

        def up_step(n, carry):
            cols = pl.ds(pl.multiple_of(n * IN_TILE, IN_TILE), IN_TILE)
            back = lax.dot_general(incoming, wo[cols, :], contract_last, preferred_element_type=f32)
            hidden[:, cols] = (back * factor[t, :, cols]).astype(bf16)
            return carry

        lax.fori_loop(0, units // IN_TILE, up_step, 0)

        def down_step(n, carry):
            cols = pl.ds(pl.multiple_of(n * OUT_TILE, OUT_TILE), OUT_TILE)
            total = lax.dot_general(hidden[...], wi[cols, :], contract_last, preferred_element_type=f32)
            total = total.reshape(tps, PAD, OUT_TILE)
            acc[:, :, cols] = total
            part[t, :, :, cols] = total.astype(bf16)
            return carry

        lax.fori_loop(0, width // OUT_TILE, down_step, 0)
        remote(part.at[t, pl.ds(theirs, places)], core_in.at[t], core_send.at[t], core_recv.at[t],
               section, partner).start()
        wait_for(core_in.at[t], core_recv.at[t])
        half[t] = (acc[pl.ds(mine, places)] + core_in[t].astype(f32)).astype(bf16)
        for k in (6, 7, 4, 5, 2, 3, 1):
            remote(half.at[t, other_place(k)], rs_in.at[t, k - 1], rs_send.at[t], rs_recv.at[t],
                   section, other_place(k) * 2 + core).start()
        if t + 1 < ticks:
            forward(x_all, t + 1, x_recv, xf_send, xf_recv)
            preact(t + 1)
        inverse_rms, normed = norm_parts(x_all[t, mine + place])
        incoming_own = own[t].astype(f32)
        total = acc[mine + place] + core_in[t, place].astype(f32)
        wait_for(rs_in.at[t], rs_recv.at[t])
        total = total + jnp.sum(rs_in[t].astype(f32), axis=0)
        scaled = total * gain_row
        inner = jnp.mean(scaled * normed, axis=-1, keepdims=True)
        result = (incoming_own + inverse_rms * (scaled - normed * inner)).astype(bf16)
        out_v[t] = result
        if t + 1 < ticks:
            @pl.when(section > 0)
            def _():
                remote(out_v.at[t], up.at[t], up_send.at[t], up_recv.at[t], below, me).start()

            @pl.when(section < sections - 1)
            def _():
                wait_for(up.at[t], up_recv.at[t])
                own[t + 1] = up[t]

            send_incoming(t + 1, own.at[t + 1])
            forward(inc_all, t + 1, ag_recv, agf_send, agf_recv)

    for t in range(ticks):
        out[t] = out_v[t, 0:rows]
    for t in range(ticks):
        wait_for(x_all.at[t, pl.ds(0, places)], x_send.at[t])
        wait_for(x_all.at[t, pl.ds(0, places - 1)], ag_send.at[t])
        wait_for(core_in.at[t], core_send.at[t])
        wait_for(rs_in.at[t], rs_send.at[t])
    for t in range(ticks - 1):
        @pl.when(section > 0)
        def _():
            wait_for(up.at[t], up_send.at[t])


def solution(mesh):
    sections, tps = mesh.shape["section"], mesh.shape["tp"]

    def body(stash, w_in, w_out, gain, plan, arriving, fresh):
        stash, w_in, w_out, arriving = stash[0], w_in[0], w_out[0], arriving[0]
        slots, rows, width = stash.shape
        ticks = plan.shape[0]
        units = w_out.shape[0]
        places = tps // 2
        vmem = pl.BlockSpec(memory_space=pltpu.VMEM)
        hbm = pl.BlockSpec(memory_space=pl.ANY)
        dma = pltpu.SemaphoreType.DMA((ticks,))
        results = pl.pallas_call(
            functools.partial(window_kernel, sections, tps, ticks),
            out_shape=jax.ShapeDtypeStruct((ticks, rows, width), bf16),
            in_specs=[pl.BlockSpec(memory_space=pltpu.SMEM), hbm, hbm, hbm, vmem, vmem, vmem],
            out_specs=vmem,
            scratch_shapes=[
                pltpu.VMEM((width, units), bf16),
                pltpu.VMEM((units, width), bf16),
                pltpu.VMEM((slots, rows, width), bf16),
                pltpu.VMEM((ticks, PAD, width), bf16),
                pltpu.VMEM((ticks, PAD, width), bf16),
                pltpu.VMEM((ticks, tps, PAD, width), bf16),
                pltpu.VMEM((ticks, tps, PAD, width), bf16),
                pltpu.VMEM((ticks, tps * PAD, units), f32),
                pltpu.VMEM((tps * PAD, units), bf16),
                pltpu.VMEM((tps, PAD, width), f32),
                pltpu.VMEM((ticks, tps, PAD, width), bf16),
                pltpu.VMEM((ticks, places, PAD, width), bf16),
                pltpu.VMEM((ticks, places, PAD, width), bf16),
                pltpu.VMEM((ticks, places - 1, PAD, width), bf16),
                pltpu.VMEM((ticks, PAD, width), bf16),
                pltpu.VMEM((ticks - 1, PAD, width), bf16),
                pltpu.SemaphoreType.DMA((3,)),
            ] + [dma] * 12 + [pltpu.SemaphoreType.DMA((ticks - 1,))] * 2,
            compiler_params=pltpu.CompilerParams(
                collective_id=0, has_side_effects=True, vmem_limit_bytes=60 * 2**20),
            name="window",
        )(plan, stash, w_in, w_out, gain, arriving, fresh)
        return results[:, None]

    placed = (
        P("section", None, "tp", None),
        P("section", None, "tp"),
        P("section", "tp", None),
        P("section", None),
        P(),
        P("section", "tp", None),
        P(None, "tp", None),
    )
    return jax.shard_map(
        body, mesh=mesh, in_specs=placed, out_specs=P(None, "section", "tp", None), check_vma=False
    )
```

```python
import functools

import jax
import jax.numpy as jnp
from jax import lax
from jax.experimental import pallas as pl
from jax.experimental.pallas import tpu as pltpu
from jax.sharding import PartitionSpec as P

epsilon = 1e-06
contract_last = (((1,), (1,)), ((), ()))
bf16, f32 = jnp.bfloat16, jnp.float32
PAD = 16
IN_TILE = 512
BLOCK = 256
LANES = 128
SUB = 8
WIRE = BLOCK + LANES
FAR_FIRST = (5, 7, 1, 3, 4, 6, 2)
FLIPPED = (5, 7, 1, 3)
NEAR = (4, 6, 2)


def packed(value):
    low = value[:, SUB:, :LANES]
    high = pltpu.roll(value[:, SUB:, LANES:], 4, 1)
    row = lax.broadcasted_iota(jnp.int32, low.shape, 1)
    return jnp.concatenate([value[:, :SUB], jnp.where(row < 4, low, high)], axis=2)


def unpacked(wire):
    wire = wire.astype(f32)
    tail = wire[:, :, BLOCK:]
    bottom = jnp.concatenate([tail, pltpu.roll(tail, 4, 1)], axis=2)
    return jnp.concatenate([wire[:, :, :BLOCK], bottom], axis=1)


def window_kernel(
    sections, tps, ticks,
    plan, stash, w_in, w_out, gain, arriving, fresh, out,
    wi, wo, picks, x_all, inc_all, factor, back_sum, hidden, acc, part, core_in, half, rs_in, out_v, pad_v,
    load_sem, x_send, x_recv, xf_send, xf_recv, ag_send, ag_recv, agf_send, agf_recv,
    core_send, core_recv, rs_send, rs_recv, up_send, up_recv, top_send,
):
    section = lax.axis_index("section")
    me = lax.axis_index("tp")
    core = lax.rem(me, 2)
    place = me // 2
    places = tps // 2
    rows, slots, width = stash.shape
    units = wo.shape[0]
    blocks = width // BLOCK
    mirror = lax.rem(section + sections // 2, sections)
    above = lax.rem(section + 1, sections)
    below = lax.rem(section + sections - 1, sections)
    mine = pl.multiple_of(core * places, places)
    theirs = pl.multiple_of((1 - core) * places, places)
    own = mine + place
    partner = me + 1 - 2 * core

    def remote(src, dst, send, recv, to_section, to_tp):
        return pltpu.make_async_remote_copy(
            src_ref=src, dst_ref=dst, send_sem=send, recv_sem=recv,
            device_id={"section": to_section, "tp": to_tp}, device_id_type=pl.DeviceIdType.MESH)

    def wait_for(ref, sem):
        pltpu.make_async_copy(ref, ref, sem).wait()

    def at_place(k):
        return lax.bitwise_xor(place, k) * 2 + core

    def cols_of(b):
        return slice(b * BLOCK, (b + 1) * BLOCK)

    loads = [
        pltpu.make_async_copy(w_in, wi, load_sem.at[0]),
        pltpu.make_async_copy(w_out, wo, load_sem.at[1]),
    ]
    loads[0].start()

    barrier = pltpu.get_barrier_semaphore()

    def greet(to_section, to_tp):
        pl.semaphore_signal(barrier, inc=1, device_id={"section": to_section, "tp": to_tp},
                            device_id_type=pl.DeviceIdType.MESH)

    for k in FAR_FIRST:
        greet(section, at_place(k))
    for k in FAR_FIRST + (0,):
        greet(mirror, at_place(k))
    for k in FLIPPED + (0,):
        greet(above, at_place(k))
        greet(below, at_place(k))
    greet(section, partner)

    pad_v[...] = jnp.zeros_like(pad_v)

    def wire_blocks(value):
        pad_v[0:rows] = value.astype(f32)
        return [packed(pad_v[:, cols_of(b)][None])[0].astype(bf16) for b in range(blocks)]

    def set_own(t, value):
        for b, block in enumerate(wire_blocks(value)):
            inc_all[t, b, own] = block

    def set_pick(t):
        slot = plan[t, mirror]
        pick = stash[:, 0, :]
        for k in range(1, slots):
            pick = jnp.where(slot == k, stash[:, k, :], pick)
        for b, block in enumerate(wire_blocks(pick)):
            picks[t, b] = block

    set_pick(0)
    set_own(0, arriving[...])
    pl.semaphore_wait(barrier, 2 * places + 2 * (1 + len(FLIPPED)))

    def send_x(t):
        for b in range(blocks):
            for k in FAR_FIRST + (0,):
                remote(picks.at[t, b], x_all.at[t, b, own], x_send.at[t], x_recv.at[t, b],
                       mirror, at_place(k)).start()

    def send_own(t, b, to_places, send):
        for k in to_places:
            remote(inc_all.at[t, b, own], inc_all.at[t, b, own], send, ag_recv.at[t, b],
                   section, at_place(k)).start()

    def forward_x(t, b):
        block = x_all.at[t, b, pl.ds(mine, places)]
        wait_for(block, x_recv.at[t, b])
        remote(block, block, xf_send.at[t], xf_recv.at[t, b], section, partner).start()

    def forward_incoming(t, b):
        wait_for(inc_all.at[t, b, pl.ds(0, places - 1)], ag_recv.at[t, b])
        block = inc_all.at[t, b, pl.ds(mine, places)]
        remote(block, block, agf_send.at[t], agf_recv.at[t, b], section, partner).start()

    gain_row = gain[...]

    def preact(t, b, scale_in, scale_out):
        values = unpacked(x_all[t, b]).reshape(tps * PAD, BLOCK)
        if scale_in is not None:
            values = values * scale_in
        inputs = (values * gain_row[:, cols_of(b)]).astype(bf16)
        for n in range(units // IN_TILE):
            cols = slice(n * IN_TILE, (n + 1) * IN_TILE)
            pre = jnp.dot(inputs, wi[cols_of(b), cols], preferred_element_type=f32)
            if b > 0:
                pre = pre + factor[:, cols]
            if b == blocks - 1:
                pre = scale_out * jnp.maximum(pre, 0.0)
            factor[:, cols] = pre

    def x_square(t, b):
        wait_for(x_all.at[t, b, pl.ds(theirs, places)], xf_recv.at[t, b])
        values = unpacked(x_all[t, b]).reshape(tps * PAD, BLOCK)
        return jnp.sum(values * values, axis=-1, keepdims=True)

    def rms_of(square):
        return lax.rsqrt(square * (1.0 / width) + epsilon)

    def first_matmul(t, b):
        wait_for(inc_all.at[t, b, pl.ds(theirs, places)], agf_recv.at[t, b])
        incoming = unpacked(inc_all[t, b]).reshape(tps * PAD, BLOCK).astype(bf16)
        for n in range(units // IN_TILE):
            cols = slice(n * IN_TILE, (n + 1) * IN_TILE)
            back = lax.dot_general(incoming, wo[cols, cols_of(b)], contract_last, preferred_element_type=f32)
            if b > 0:
                back = back + back_sum[:, cols]
            if b == blocks - 1:
                hidden[:, cols] = (back * factor[:, cols]).astype(bf16)
            else:
                back_sum[:, cols] = back

    def second_matmul(t, b):
        total = lax.dot_general(hidden[...], wi[cols_of(b), :], contract_last, preferred_element_type=f32)
        total = packed(total.reshape(tps, PAD, BLOCK))
        acc[b] = total
        part[t, b] = total.astype(bf16)
        remote(part.at[t, b, pl.ds(theirs, places)], core_in.at[t, b], core_send.at[t], core_recv.at[t, b],
               section, partner).start()

    def scatter(t, b):
        wait_for(core_in.at[t, b], core_recv.at[t, b])
        half[t, b] = (acc[b, pl.ds(mine, places)] + core_in[t, b].astype(f32)).astype(bf16)
        for k in FAR_FIRST:
            remote(half.at[t, b, lax.bitwise_xor(place, k)], rs_in.at[t, b, k - 1], rs_send.at[t], rs_recv.at[t, b],
                   section, at_place(k)).start()

    send_x(0)
    for b in range(blocks):
        send_own(0, b, FAR_FIRST, ag_send.at[0])
    loads[1].start()
    for t in range(1, ticks):
        set_pick(t)

    @pl.when(section == sections - 1)
    def _():
        for t in range(1, ticks):
            set_own(t, fresh[:, t - 1, :])

    forward_x(0, 0)
    forward_x(0, 1)
    loads[0].wait()
    for b in range(blocks):
        if b + 2 < blocks:
            forward_x(0, b + 2)
        else:
            forward_incoming(0, b + 2 - blocks)
        square = x_square(0, b) if b == 0 else square + x_square(0, b)
        preact(0, b, None, 2.0 * rms_of(square) if b == blocks - 1 else None)

    loads[1].wait()
    for t in range(ticks):
        if t > 0:
            forward_incoming(t, 0)
            forward_incoming(t, 1)
        for b in range(blocks):
            first_matmul(t, b)
            if b + 2 < blocks:
                forward_incoming(t, b + 2)
        second_matmul(t, 0)
        second_matmul(t, 1)
        for b in range(2, blocks):
            second_matmul(t, b)
            scatter(t, b - 2)
        scatter(t, blocks - 2)
        scatter(t, blocks - 1)
        if t + 1 < ticks:
            send_x(t + 1)
        values = jnp.concatenate([unpacked(x_all[t, b, pl.ds(own, 1)])[0] for b in range(blocks)], axis=1)
        inverse_rms = lax.rsqrt(jnp.mean(values * values, axis=-1, keepdims=True) + epsilon)
        normed = values * inverse_rms
        incoming = jnp.concatenate([unpacked(inc_all[t, b, pl.ds(own, 1)])[0] for b in range(blocks)], axis=1)
        scaled = []
        for b in range(blocks):
            wait_for(rs_in.at[t, b], rs_recv.at[t, b])
            total = (acc[b, pl.ds(own, 1)] + core_in[t, b, pl.ds(place, 1)].astype(f32)
                     + jnp.sum(rs_in[t, b].astype(f32), axis=0, keepdims=True))
            scaled.append(unpacked(total)[0] * gain_row[:, cols_of(b)])
        scaled = jnp.concatenate(scaled, axis=1)
        inner = jnp.mean(scaled * normed, axis=-1, keepdims=True)
        result = incoming + inverse_rms * (scaled - normed * inner)
        if t + 1 < ticks:
            for b in range(blocks):
                out_v[t, b] = packed(result[:, cols_of(b)][None])[0].astype(bf16)

            @pl.when(section > 0)
            def _():
                for b in range(blocks):
                    remote(out_v.at[t, b], inc_all.at[t + 1, b, own], up_send.at[t], up_recv.at[t, b], below, me).start()
                    for k in FLIPPED:
                        remote(out_v.at[t, b], inc_all.at[t + 1, b, own], up_send.at[t], ag_recv.at[t + 1, b],
                               below, at_place(k)).start()

            @pl.when(section == sections - 1)
            def _():
                for b in range(blocks):
                    send_own(t + 1, b, FLIPPED, top_send.at[t])

        out[t] = result[0:rows].astype(bf16)
        if t + 1 < ticks:
            for b in range(blocks):
                forward_x(t + 1, b)
            for b in range(blocks):
                @pl.when(section < sections - 1)
                def _():
                    wait_for(inc_all.at[t + 1, b, own], up_recv.at[t, b])

                send_own(t + 1, b, NEAR, ag_send.at[t + 1])

            square = x_square(t + 1, 0)
            for b in range(1, blocks):
                square = square + x_square(t + 1, b)
            for b in range(blocks):
                preact(t + 1, b, rms_of(square), 2.0)

    def sent(t, copies, sem):
        wait_for(inc_all.at[t, pl.ds(0, blocks), pl.ds(0, copies)], sem)

    for t in range(ticks):
        wait_for(x_all.at[t, pl.ds(0, blocks), pl.ds(0, places)], x_send.at[t])
        wait_for(x_all.at[t, pl.ds(0, blocks), pl.ds(0, places)], xf_send.at[t])
        sent(t, len(FAR_FIRST) if t == 0 else len(NEAR), ag_send.at[t])
        sent(t, places, agf_send.at[t])
        wait_for(core_in.at[t], core_send.at[t])
        wait_for(rs_in.at[t], rs_send.at[t])
    for t in range(ticks - 1):
        @pl.when(section > 0)
        def _():
            sent(t, 1 + len(FLIPPED), up_send.at[t])

        @pl.when(section == sections - 1)
        def _():
            sent(t, len(FLIPPED), top_send.at[t])


def solution(mesh):
    sections, tps = mesh.shape["section"], mesh.shape["tp"]

    def body(stash, w_in, w_out, gain, plan, arriving, fresh):
        stash, w_in, w_out, arriving = stash[0], w_in[0], w_out[0], arriving[0]
        stash, fresh = jnp.swapaxes(stash, 0, 1), jnp.swapaxes(fresh, 0, 1)
        rows, slots, width = stash.shape
        ticks = plan.shape[0]
        units = w_out.shape[0]
        places = tps // 2
        blocks = width // BLOCK
        vmem = pl.BlockSpec(memory_space=pltpu.VMEM)
        hbm = pl.BlockSpec(memory_space=pl.ANY)
        each = pltpu.SemaphoreType.DMA((ticks,))
        each_block = pltpu.SemaphoreType.DMA((ticks, blocks))
        results = pl.pallas_call(
            functools.partial(window_kernel, sections, tps, ticks),
            out_shape=jax.ShapeDtypeStruct((ticks, rows, width), bf16),
            in_specs=[pl.BlockSpec(memory_space=pltpu.SMEM), vmem, hbm, hbm, vmem, vmem, vmem],
            out_specs=vmem,
            scratch_shapes=[
                pltpu.VMEM((width, units), bf16),
                pltpu.VMEM((units, width), bf16),
                pltpu.VMEM((ticks, blocks, SUB, WIRE), bf16),
                pltpu.VMEM((ticks, blocks, tps, SUB, WIRE), bf16),
                pltpu.VMEM((ticks, blocks, tps, SUB, WIRE), bf16),
                pltpu.VMEM((tps * PAD, units), f32),
                pltpu.VMEM((tps * PAD, units), f32),
                pltpu.VMEM((tps * PAD, units), bf16),
                pltpu.VMEM((blocks, tps, SUB, WIRE), f32),
                pltpu.VMEM((ticks, blocks, tps, SUB, WIRE), bf16),
                pltpu.VMEM((ticks, blocks, places, SUB, WIRE), bf16),
                pltpu.VMEM((ticks, blocks, places, SUB, WIRE), bf16),
                pltpu.VMEM((ticks, blocks, places - 1, SUB, WIRE), bf16),
                pltpu.VMEM((ticks, blocks, SUB, WIRE), bf16),
                pltpu.VMEM((PAD, width), f32),
                pltpu.SemaphoreType.DMA((2,)),
                each, each_block, each, each_block,
                each, each_block, each, each_block,
                each, each_block, each, each_block,
                each, each_block, each,
            ],
            compiler_params=pltpu.CompilerParams(
                collective_id=0, has_side_effects=True, vmem_limit_bytes=60 * 2**20),
            name="window",
        )(plan, stash, w_in, w_out, gain, arriving, fresh)
        return results[:, None]

    placed = (
        P("section", None, "tp", None),
        P("section", None, "tp"),
        P("section", "tp", None),
        P("section", None),
        P(),
        P("section", "tp", None),
        P(None, "tp", None),
    )
    return jax.shard_map(
        body, mesh=mesh, in_specs=placed, out_specs=P(None, "section", "tp", None), check_vma=False
    )
```

```python
import functools

import jax
import jax.numpy as jnp
from jax import lax
from jax.experimental import pallas as pl
from jax.experimental.pallas import tpu as pltpu
from jax.sharding import PartitionSpec as P

epsilon = 1e-06
contract_last = (((1,), (1,)), ((), ()))
bf16, f32 = jnp.bfloat16, jnp.float32
PAD = 16
IN_TILE = 512
BLOCK = 256
LANES = 128
SUB = 8
WIRE = BLOCK + LANES
FAR_FIRST = (5, 7, 1, 3, 4, 6, 2)
FLIPPED = (5, 7, 1, 3)
NEAR = (4, 6, 2)
AHEAD = 3


def packed(value):
    low = value[:, SUB:, :LANES]
    high = pltpu.roll(value[:, SUB:, LANES:], 4, 1)
    row = lax.broadcasted_iota(jnp.int32, low.shape, 1)
    return jnp.concatenate([value[:, :SUB], jnp.where(row < 4, low, high)], axis=2)


def unpacked(wire):
    wire = wire.astype(f32)
    tail = wire[:, :, BLOCK:]
    bottom = jnp.concatenate([tail, pltpu.roll(tail, 4, 1)], axis=2)
    return jnp.concatenate([wire[:, :, :BLOCK], bottom], axis=1)


def window_kernel(
    sections, tps, ticks,
    plan_in, stash_in, w_in, w_out, gain_in, arriving_in, fresh_in, out,
    plan, stash, gain, arriving, fresh, wi, wo, picks, x_all, inc_all, factor, back_sum, hidden, raw, acc, part, core_in, half, rs_in, out_v, pad_v,
    load_sem, x_send, x_recv, xf_send, xf_recv, ag_send, ag_recv, agf_send, agf_recv,
    core_send, core_recv, rs_send, rs_recv, up_send, up_recv, top_send,
):
    section = lax.axis_index("section")
    me = lax.axis_index("tp")
    core = lax.rem(me, 2)
    place = me // 2
    places = tps // 2
    rows, slots, width = stash.shape
    units = wo.shape[0]
    blocks = width // BLOCK
    mirror = lax.rem(section + sections // 2, sections)
    above = lax.rem(section + 1, sections)
    below = lax.rem(section + sections - 1, sections)
    mine = pl.multiple_of(core * places, places)
    theirs = pl.multiple_of((1 - core) * places, places)
    own = mine + place
    partner = me + 1 - 2 * core

    def remote(src, dst, send, recv, to_section, to_tp):
        return pltpu.make_async_remote_copy(
            src_ref=src, dst_ref=dst, send_sem=send, recv_sem=recv,
            device_id={"section": to_section, "tp": to_tp}, device_id_type=pl.DeviceIdType.MESH)

    def wait_for(ref, sem):
        pltpu.make_async_copy(ref, ref, sem).wait()

    def at_place(k):
        return lax.bitwise_xor(place, k) * 2 + core

    def cols_of(b):
        return slice(b * BLOCK, (b + 1) * BLOCK)

    barrier = pltpu.get_barrier_semaphore()

    def greet(to_section, to_tp):
        pl.semaphore_signal(barrier, inc=1, device_id={"section": to_section, "tp": to_tp},
                            device_id_type=pl.DeviceIdType.MESH)

    for k in FAR_FIRST:
        greet(section, at_place(k))
    for k in FAR_FIRST + (0,):
        greet(mirror, at_place(k))
    for k in FLIPPED + (0,):
        greet(above, at_place(k))
        greet(below, at_place(k))
    greet(section, partner)

    pairs = ((plan_in, plan), (stash_in, stash), (arriving_in, arriving), (gain_in, gain), (fresh_in, fresh), (w_in, wi), (w_out, wo))
    loads = [pltpu.make_async_copy(src, dst, load_sem.at[n]) for n, (src, dst) in enumerate(pairs)]
    for load in loads[:-1]:
        load.start()
    pad_v[...] = jnp.zeros_like(pad_v)
    for load in loads[:3]:
        load.wait()

    def wire_blocks(value):
        pad_v[0:rows] = value.astype(f32)
        return [packed(pad_v[:, cols_of(b)][None])[0].astype(bf16) for b in range(blocks)]

    def set_own(t, value):
        for b, block in enumerate(wire_blocks(value)):
            inc_all[t, b, own] = block

    def set_pick(t):
        slot = plan[t, mirror]
        pick = stash[:, 0, :]
        for k in range(1, slots):
            pick = jnp.where(slot == k, stash[:, k, :], pick)
        for b, block in enumerate(wire_blocks(pick)):
            picks[t, b] = block

    set_pick(0)
    set_own(0, arriving[...])
    pl.semaphore_wait(barrier, 2 * places + 2 * (1 + len(FLIPPED)))

    def send_x(t):
        for b in range(blocks):
            for k in FAR_FIRST + (0,):
                remote(picks.at[t, b], x_all.at[t, b, own], x_send.at[t], x_recv.at[t, b],
                       mirror, at_place(k)).start()

    def send_own(t, b, to_places, send):
        for k in to_places:
            remote(inc_all.at[t, b, own], inc_all.at[t, b, own], send, ag_recv.at[t, b],
                   section, at_place(k)).start()

    def forward_x(t, b):
        block = x_all.at[t, b, pl.ds(mine, places)]
        wait_for(block, x_recv.at[t, b])
        remote(block, block, xf_send.at[t], xf_recv.at[t, b], section, partner).start()

    def forward_incoming(t, b):
        wait_for(inc_all.at[t, b, pl.ds(0, places - 1)], ag_recv.at[t, b])
        block = inc_all.at[t, b, pl.ds(mine, places)]
        remote(block, block, agf_send.at[t], agf_recv.at[t, b], section, partner).start()

    def preact(t, b, scale_in, scale_out):
        values = unpacked(x_all[t, b]).reshape(tps * PAD, BLOCK)
        if scale_in is not None:
            values = values * scale_in
        inputs = (values * gain[:, cols_of(b)]).astype(bf16)
        for n in range(units // IN_TILE):
            cols = slice(n * IN_TILE, (n + 1) * IN_TILE)
            pre = jnp.dot(inputs, wi[cols_of(b), cols], preferred_element_type=f32)
            if b > 0:
                pre = pre + factor[:, cols]
            if b == blocks - 1:
                pre = scale_out * jnp.maximum(pre, 0.0)
            factor[:, cols] = pre

    def x_square(t, b):
        wait_for(x_all.at[t, b, pl.ds(theirs, places)], xf_recv.at[t, b])
        values = unpacked(x_all[t, b]).reshape(tps * PAD, BLOCK)
        return jnp.sum(values * values, axis=-1, keepdims=True)

    def rms_of(square):
        return lax.rsqrt(square * (1.0 / width) + epsilon)

    def first_matmul(t, b):
        wait_for(inc_all.at[t, b, pl.ds(theirs, places)], agf_recv.at[t, b])
        incoming = unpacked(inc_all[t, b]).reshape(tps * PAD, BLOCK).astype(bf16)
        for n in range(units // IN_TILE):
            cols = slice(n * IN_TILE, (n + 1) * IN_TILE)
            back = lax.dot_general(incoming, wo[cols, cols_of(b)], contract_last, preferred_element_type=f32)
            if b > 0:
                back = back + back_sum[:, cols]
            if b == blocks - 1:
                hidden[:, cols] = (back * factor[:, cols]).astype(bf16)
            else:
                back_sum[:, cols] = back

    def second_matmul(b):
        raw[b] = lax.dot_general(hidden[...], wi[cols_of(b), :], contract_last, preferred_element_type=f32)

    def pack_part(t, b):
        total = packed(raw[b].reshape(tps, PAD, BLOCK))
        acc[b] = total
        part[t, b] = total.astype(bf16)

    def send_part(t, b):
        remote(part.at[t, b, pl.ds(theirs, places)], core_in.at[t, b], core_send.at[t], core_recv.at[t, b],
               section, partner).start()

    def take_part(t, b):
        wait_for(core_in.at[t, b], core_recv.at[t, b])

    def pack_half(t, b):
        half[t, b] = (acc[b, pl.ds(mine, places)] + core_in[t, b].astype(f32)).astype(bf16)

    def scatter(t, b):
        for k in FAR_FIRST:
            remote(half.at[t, b, lax.bitwise_xor(place, k)], rs_in.at[t, b, k - 1], rs_send.at[t], rs_recv.at[t, b],
                   section, at_place(k)).start()

    send_x(0)
    for b in range(blocks):
        send_own(0, b, FAR_FIRST, ag_send.at[0])
    loads[6].start()
    for t in range(1, ticks):
        set_pick(t)
    loads[3].wait()
    loads[4].wait()

    @pl.when(section == sections - 1)
    def _():
        for t in range(1, ticks):
            set_own(t, fresh[:, t - 1, :])

    for b in range(AHEAD):
        forward_x(0, b)
    loads[5].wait()
    for b in range(blocks):
        square = x_square(0, b) if b == 0 else square + x_square(0, b)
        preact(0, b, None, 2.0 * rms_of(square) if b == blocks - 1 else None)
        if b + AHEAD < blocks:
            forward_x(0, b + AHEAD)
        else:
            forward_incoming(0, b + AHEAD - blocks)
    loads[6].wait()
    for t in range(ticks):
        if t > 0:
            for b in range(AHEAD):
                forward_incoming(t, b)
        for b in range(blocks):
            first_matmul(t, b)
            if b + AHEAD < blocks:
                forward_incoming(t, b + AHEAD)
        second_matmul(0)
        for b in range(1, blocks):
            second_matmul(b)
            pack_part(t, b - 1)
            if b > 2:
                pack_half(t, b - 3)
            send_part(t, b - 1)
            if b > 2:
                scatter(t, b - 3)
            if b > 1 and b < blocks - 1:
                take_part(t, b - 2)
        pack_part(t, blocks - 1)
        send_part(t, blocks - 1)
        for b in range(blocks - 3, blocks):
            take_part(t, b)
            pack_half(t, b)
            scatter(t, b)
        if t + 1 < ticks:
            send_x(t + 1)
        values = jnp.concatenate([unpacked(x_all[t, b, pl.ds(own, 1)])[0] for b in range(blocks)], axis=1)
        inverse_rms = lax.rsqrt(jnp.mean(values * values, axis=-1, keepdims=True) + epsilon)
        normed = values * inverse_rms
        incoming = jnp.concatenate([unpacked(inc_all[t, b, pl.ds(own, 1)])[0] for b in range(blocks)], axis=1)
        scaled = []
        for b in range(blocks):
            wait_for(rs_in.at[t, b], rs_recv.at[t, b])
            total = (acc[b, pl.ds(own, 1)] + core_in[t, b, pl.ds(place, 1)].astype(f32)
                     + jnp.sum(rs_in[t, b].astype(f32), axis=0, keepdims=True))
            scaled.append(unpacked(total)[0] * gain[:, cols_of(b)])
        scaled = jnp.concatenate(scaled, axis=1)
        inner = jnp.mean(scaled * normed, axis=-1, keepdims=True)
        result = incoming + inverse_rms * (scaled - normed * inner)
        if t + 1 < ticks:
            for b in range(blocks):
                out_v[t, b] = packed(result[:, cols_of(b)][None])[0].astype(bf16)

            @pl.when(section > 0)
            def _():
                for b in range(blocks):
                    remote(out_v.at[t, b], inc_all.at[t + 1, b, own], up_send.at[t], up_recv.at[t, b], below, me).start()
                    for k in FLIPPED:
                        remote(out_v.at[t, b], inc_all.at[t + 1, b, own], up_send.at[t], ag_recv.at[t + 1, b],
                               below, at_place(k)).start()

            @pl.when(section == sections - 1)
            def _():
                for b in range(blocks):
                    send_own(t + 1, b, FLIPPED, top_send.at[t])

        out[t] = result[0:rows].astype(bf16)
        if t + 1 < ticks:
            for b in range(blocks):
                forward_x(t + 1, b)
            for b in range(blocks):
                @pl.when(section < sections - 1)
                def _():
                    wait_for(inc_all.at[t + 1, b, own], up_recv.at[t, b])

                send_own(t + 1, b, NEAR, ag_send.at[t + 1])

            square = x_square(t + 1, 0)
            for b in range(1, blocks):
                square = square + x_square(t + 1, b)
            for b in range(blocks):
                preact(t + 1, b, rms_of(square), 2.0)

    def sent(t, copies, sem):
        wait_for(inc_all.at[t, pl.ds(0, blocks), pl.ds(0, copies)], sem)

    for t in range(ticks):
        wait_for(x_all.at[t, pl.ds(0, blocks), pl.ds(0, places)], x_send.at[t])
        wait_for(x_all.at[t, pl.ds(0, blocks), pl.ds(0, places)], xf_send.at[t])
        sent(t, len(FAR_FIRST) if t == 0 else len(NEAR), ag_send.at[t])
        sent(t, places, agf_send.at[t])
        wait_for(core_in.at[t], core_send.at[t])
        wait_for(rs_in.at[t], rs_send.at[t])
    for t in range(ticks - 1):
        @pl.when(section > 0)
        def _():
            sent(t, 1 + len(FLIPPED), up_send.at[t])

        @pl.when(section == sections - 1)
        def _():
            sent(t, len(FLIPPED), top_send.at[t])


def solution(mesh):
    sections, tps = mesh.shape["section"], mesh.shape["tp"]

    def body(stash, w_in, w_out, gain, plan, arriving, fresh):
        stash, w_in, w_out, arriving = stash[0], w_in[0], w_out[0], arriving[0]
        stash, fresh = jnp.swapaxes(stash, 0, 1), jnp.swapaxes(fresh, 0, 1)
        rows, slots, width = stash.shape
        ticks = plan.shape[0]
        units = w_out.shape[0]
        places = tps // 2
        blocks = width // BLOCK
        vmem = pl.BlockSpec(memory_space=pltpu.VMEM)
        hbm = pl.BlockSpec(memory_space=pl.ANY)
        each = pltpu.SemaphoreType.DMA((ticks,))
        each_block = pltpu.SemaphoreType.DMA((ticks, blocks))
        results = pl.pallas_call(
            functools.partial(window_kernel, sections, tps, ticks),
            out_shape=pltpu.VMEM((ticks, rows, width), bf16),
            in_specs=[hbm] * 7,
            out_specs=vmem,
            scratch_shapes=[
                pltpu.SMEM(plan.shape, plan.dtype),
                pltpu.VMEM(stash.shape, bf16),
                pltpu.VMEM(gain.shape, f32),
                pltpu.VMEM(arriving.shape, bf16),
                pltpu.VMEM(fresh.shape, bf16),
                pltpu.VMEM((width, units), bf16),
                pltpu.VMEM((units, width), bf16),
                pltpu.VMEM((ticks, blocks, SUB, WIRE), bf16),
                pltpu.VMEM((ticks, blocks, tps, SUB, WIRE), bf16),
                pltpu.VMEM((ticks, blocks, tps, SUB, WIRE), bf16),
                pltpu.VMEM((tps * PAD, units), f32),
                pltpu.VMEM((tps * PAD, units), f32),
                pltpu.VMEM((tps * PAD, units), bf16),
                pltpu.VMEM((blocks, tps * PAD, BLOCK), f32),
                pltpu.VMEM((blocks, tps, SUB, WIRE), f32),
                pltpu.VMEM((ticks, blocks, tps, SUB, WIRE), bf16),
                pltpu.VMEM((ticks, blocks, places, SUB, WIRE), bf16),
                pltpu.VMEM((ticks, blocks, places, SUB, WIRE), bf16),
                pltpu.VMEM((ticks, blocks, places - 1, SUB, WIRE), bf16),
                pltpu.VMEM((ticks, blocks, SUB, WIRE), bf16),
                pltpu.VMEM((PAD, width), f32),
                pltpu.SemaphoreType.DMA((7,)),
                each, each_block, each, each_block,
                each, each_block, each, each_block,
                each, each_block, each, each_block,
                each, each_block, each,
            ],
            compiler_params=pltpu.CompilerParams(
                collective_id=0, has_side_effects=True, vmem_limit_bytes=60 * 2**20),
            name="window",
        )(plan, stash, w_in, w_out, gain, arriving, fresh)
        return results[:, None]

    placed = (
        P("section", None, "tp", None),
        P("section", None, "tp"),
        P("section", "tp", None),
        P("section", None),
        P(),
        P("section", "tp", None),
        P(None, "tp", None),
    )
    return jax.shard_map(
        body, mesh=mesh, in_specs=placed, out_specs=P(None, "section", "tp", None), check_vma=False
    )
```

```python
import functools

import jax
import jax.numpy as jnp
from jax import lax
from jax.experimental import pallas as pl
from jax.experimental.pallas import tpu as pltpu
from jax.sharding import PartitionSpec as P

epsilon = 1e-06
contract_last = (((1,), (1,)), ((), ()))
bf16, f32 = jnp.bfloat16, jnp.float32
PAD = 16
IN_TILE = 512
BLOCK = 256
LANES = 128
SUB = 8
WIRE = BLOCK + LANES
FAR_FIRST = (5, 7, 1, 3, 4, 6, 2)
FLIPPED = (5, 7, 3)
NEAR = (1, 4, 6, 2)
AHEAD = 3


def packed(value):
    low = value[:, SUB:, :LANES]
    high = pltpu.roll(value[:, SUB:, LANES:], 4, 1)
    row = lax.broadcasted_iota(jnp.int32, low.shape, 1)
    return jnp.concatenate([value[:, :SUB], jnp.where(row < 4, low, high)], axis=2)


def unpacked(wire):
    wire = wire.astype(f32)
    tail = wire[:, :, BLOCK:]
    bottom = jnp.concatenate([tail, pltpu.roll(tail, 4, 1)], axis=2)
    return jnp.concatenate([wire[:, :, :BLOCK], bottom], axis=1)


def window_kernel(
    sections, tps, ticks,
    plan_in, stash_in, w_in, w_out, gain_in, arriving_in, fresh_in, out,
    plan, stash, gain, arriving, fresh, wi, wo, picks, x_all, inc_all, factor, back_sum, hidden, raw, acc, part, core_in, half, rs_in, out_v, pad_v,
    load_sem, x_send, x_recv, xf_send, xf_recv, ag_send, ag_recv, agf_send, agf_recv,
    core_send, core_recv, rs_send, rs_recv, up_send, up_recv, top_send,
):
    section = lax.axis_index("section")
    me = lax.axis_index("tp")
    core = lax.rem(me, 2)
    place = me // 2
    places = tps // 2
    rows, slots, width = stash.shape
    units = wo.shape[0]
    blocks = width // BLOCK
    mirror = lax.rem(section + sections // 2, sections)
    above = lax.rem(section + 1, sections)
    below = lax.rem(section + sections - 1, sections)
    mine = pl.multiple_of(core * places, places)
    theirs = pl.multiple_of((1 - core) * places, places)
    own = mine + place
    partner = me + 1 - 2 * core

    def remote(src, dst, send, recv, to_section, to_tp):
        return pltpu.make_async_remote_copy(
            src_ref=src, dst_ref=dst, send_sem=send, recv_sem=recv,
            device_id={"section": to_section, "tp": to_tp}, device_id_type=pl.DeviceIdType.MESH)

    def wait_for(ref, sem):
        pltpu.make_async_copy(ref, ref, sem).wait()

    def at_place(k):
        return lax.bitwise_xor(place, k) * 2 + core

    def cols_of(b):
        return slice(b * BLOCK, (b + 1) * BLOCK)

    barrier = pltpu.get_barrier_semaphore()

    def greet(to_section, to_tp):
        pl.semaphore_signal(barrier, inc=1, device_id={"section": to_section, "tp": to_tp},
                            device_id_type=pl.DeviceIdType.MESH)

    for k in FAR_FIRST:
        greet(section, at_place(k))
    for k in FAR_FIRST + (0,):
        greet(mirror, at_place(k))
    for k in FLIPPED + (0,):
        greet(above, at_place(k))
        greet(below, at_place(k))
    greet(section, partner)

    pairs = ((plan_in, plan), (stash_in, stash), (arriving_in, arriving), (gain_in, gain), (fresh_in, fresh), (w_in, wi), (w_out, wo))
    loads = [pltpu.make_async_copy(src, dst, load_sem.at[n]) for n, (src, dst) in enumerate(pairs)]
    for load in loads[:-1]:
        load.start()
    pad_v[...] = jnp.zeros_like(pad_v)
    for load in loads[:3]:
        load.wait()

    def wire_blocks(value):
        pad_v[0:rows] = value.astype(f32)
        return [packed(pad_v[:, cols_of(b)][None])[0].astype(bf16) for b in range(blocks)]

    def set_own(t, value):
        for b, block in enumerate(wire_blocks(value)):
            inc_all[t, b, own] = block

    def set_pick(t):
        slot = plan[t, mirror]
        pick = stash[:, 0, :]
        for k in range(1, slots):
            pick = jnp.where(slot == k, stash[:, k, :], pick)
        for b, block in enumerate(wire_blocks(pick)):
            picks[t, b] = block

    set_pick(0)
    set_own(0, arriving[...])
    pl.semaphore_wait(barrier, 2 * places + 2 * (1 + len(FLIPPED)))

    def send_x(t, parts):
        for b in parts:
            for k in FAR_FIRST + (0,):
                remote(picks.at[t, b], x_all.at[t, b, own], x_send.at[t], x_recv.at[t, b],
                       mirror, at_place(k)).start()

    def send_x_whole(t):
        for k in FAR_FIRST + (0,):
            remote(picks.at[t], x_all.at[t, pl.ds(0, blocks), own], x_send.at[t], x_recv.at[t, 0],
                   mirror, at_place(k)).start()

    def forward_x_whole(t):
        block = x_all.at[t, pl.ds(0, blocks), pl.ds(mine, places)]
        wait_for(block, x_recv.at[t, 0])
        remote(block, block, xf_send.at[t], xf_recv.at[t, 0], section, partner).start()

    def send_own(t, b, to_places, send):
        for k in to_places:
            remote(inc_all.at[t, b, own], inc_all.at[t, b, own], send, ag_recv.at[t, b],
                   section, at_place(k)).start()

    def forward_x(t, b):
        block = x_all.at[t, b, pl.ds(mine, places)]
        wait_for(block, x_recv.at[t, b])
        remote(block, block, xf_send.at[t], xf_recv.at[t, b], section, partner).start()

    def forward_incoming(t, b):
        wait_for(inc_all.at[t, b, pl.ds(0, places - 1)], ag_recv.at[t, b])
        block = inc_all.at[t, b, pl.ds(mine, places)]
        remote(block, block, agf_send.at[t], agf_recv.at[t, b], section, partner).start()

    def preact(t, b, scale_in, scale_out):
        values = unpacked(x_all[t, b]).reshape(tps * PAD, BLOCK)
        if scale_in is not None:
            values = values * scale_in
        inputs = (values * gain[:, cols_of(b)]).astype(bf16)
        for n in range(units // IN_TILE):
            cols = slice(n * IN_TILE, (n + 1) * IN_TILE)
            pre = jnp.dot(inputs, wi[cols_of(b), cols], preferred_element_type=f32)
            if b > 0:
                pre = pre + factor[:, cols]
            if b == blocks - 1:
                pre = scale_out * jnp.maximum(pre, 0.0)
            factor[:, cols] = pre

    def x_square(t, b):
        wait_for(x_all.at[t, b, pl.ds(theirs, places)], xf_recv.at[t, b])
        return row_square(t, b)

    def row_square(t, b):
        values = unpacked(x_all[t, b]).reshape(tps * PAD, BLOCK)
        return jnp.sum(values * values, axis=-1, keepdims=True)

    def rms_of(square):
        return lax.rsqrt(square * (1.0 / width) + epsilon)

    def first_matmul(t, b):
        wait_for(inc_all.at[t, b, pl.ds(theirs, places)], agf_recv.at[t, b])
        incoming = unpacked(inc_all[t, b]).reshape(tps * PAD, BLOCK).astype(bf16)
        for n in range(units // IN_TILE):
            cols = slice(n * IN_TILE, (n + 1) * IN_TILE)
            back = lax.dot_general(incoming, wo[cols, cols_of(b)], contract_last, preferred_element_type=f32)
            if b > 0:
                back = back + back_sum[:, cols]
            if b == blocks - 1:
                hidden[:, cols] = (back * factor[:, cols]).astype(bf16)
            else:
                back_sum[:, cols] = back

    def second_matmul(b):
        raw[b] = lax.dot_general(hidden[...], wi[cols_of(b), :], contract_last, preferred_element_type=f32)

    def pack_part(t, b):
        total = packed(raw[b].reshape(tps, PAD, BLOCK))
        acc[b] = total
        part[t, b] = total.astype(bf16)

    def send_part(t, b):
        remote(part.at[t, b, pl.ds(theirs, places)], core_in.at[t, b], core_send.at[t], core_recv.at[t, b],
               section, partner).start()

    def take_part(t, b):
        wait_for(core_in.at[t, b], core_recv.at[t, b])

    def pack_half(t, b):
        half[t, b] = (acc[b, pl.ds(mine, places)] + core_in[t, b].astype(f32)).astype(bf16)

    def scatter(t, b):
        for k in FAR_FIRST:
            remote(half.at[t, b, lax.bitwise_xor(place, k)], rs_in.at[t, b, k - 1], rs_send.at[t], rs_recv.at[t, b],
                   section, at_place(k)).start()

    send_x(0, range(blocks))
    for b in range(blocks):
        send_own(0, b, FAR_FIRST, ag_send.at[0])
    loads[6].start()
    for t in range(1, ticks):
        set_pick(t)
    loads[3].wait()
    loads[4].wait()

    @pl.when(section == sections - 1)
    def _():
        for t in range(1, ticks):
            set_own(t, fresh[:, t - 1, :])

    for b in range(AHEAD):
        forward_x(0, b)
    loads[5].wait()
    for b in range(blocks):
        square = x_square(0, b) if b == 0 else square + x_square(0, b)
        preact(0, b, None, 2.0 * rms_of(square) if b == blocks - 1 else None)
        if b + AHEAD < blocks:
            forward_x(0, b + AHEAD)
        else:
            forward_incoming(0, b + AHEAD - blocks)
    loads[6].wait()

    def tick(t, carry):
        more = t + 1 < ticks
        for b in range(blocks):
            first_matmul(t, b)
            if b + AHEAD < blocks:
                forward_incoming(t, b + AHEAD)
            if b == 0:
                @pl.when(more)
                def _():
                    send_x_whole(t + 1)
        second_matmul(0)
        for b in range(1, blocks):
            second_matmul(b)
            pack_part(t, b - 1)
            if b > 2:
                pack_half(t, b - 3)
            send_part(t, b - 1)
            if b > 2:
                scatter(t, b - 3)
            if b > 1 and b < blocks - 1:
                take_part(t, b - 2)
        pack_part(t, blocks - 1)
        send_part(t, blocks - 1)
        for b in range(blocks - 3, blocks):
            take_part(t, b)
            pack_half(t, b)
            scatter(t, b)
        values = jnp.concatenate([unpacked(x_all[t, b, pl.ds(own, 1)])[0] for b in range(blocks)], axis=1)
        inverse_rms = lax.rsqrt(jnp.mean(values * values, axis=-1, keepdims=True) + epsilon)
        normed = values * inverse_rms
        incoming = jnp.concatenate([unpacked(inc_all[t, b, pl.ds(own, 1)])[0] for b in range(blocks)], axis=1)
        scaled = []
        for b in range(blocks):
            wait_for(rs_in.at[t, b], rs_recv.at[t, b])
            total = (acc[b, pl.ds(own, 1)] + core_in[t, b, pl.ds(place, 1)].astype(f32)
                     + jnp.sum(rs_in[t, b].astype(f32), axis=0, keepdims=True))
            scaled.append(unpacked(total)[0] * gain[:, cols_of(b)])
        scaled = jnp.concatenate(scaled, axis=1)
        inner = jnp.mean(scaled * normed, axis=-1, keepdims=True)
        result = incoming + inverse_rms * (scaled - normed * inner)
        for b in range(blocks):
            out_v[t, b] = packed(result[:, cols_of(b)][None])[0].astype(bf16)

        @pl.when(jnp.logical_and(more, section > 0))
        def _():
            for b in range(blocks):
                remote(out_v.at[t, b], inc_all.at[t + 1, b, own], up_send.at[t], up_recv.at[t, b], below, me).start()
            for b in range(blocks):
                for k in FLIPPED:
                    remote(out_v.at[t, b], inc_all.at[t + 1, b, own], up_send.at[t], ag_recv.at[t + 1, b],
                           below, at_place(k)).start()

        @pl.when(jnp.logical_and(more, section == sections - 1))
        def _():
            for b in range(blocks):
                send_own(t + 1, b, FLIPPED, top_send.at[t])

        out[t] = result[0:rows].astype(bf16)

        @pl.when(more)
        def _():
            forward_x_whole(t + 1)
            for b in range(blocks):
                @pl.when(section < sections - 1)
                def _():
                    wait_for(inc_all.at[t + 1, b, own], up_recv.at[t, b])

                send_own(t + 1, b, NEAR, ag_send.at[t + 1])

            wait_for(x_all.at[t + 1, pl.ds(0, blocks), pl.ds(theirs, places)], xf_recv.at[t + 1, 0])
            square = row_square(t + 1, 0)
            for b in range(1, blocks):
                square = square + row_square(t + 1, b)
            for b in range(blocks):
                preact(t + 1, b, rms_of(square), 2.0)
            for b in range(AHEAD):
                forward_incoming(t + 1, b)

        return carry

    lax.fori_loop(0, ticks, tick, 0)

    def sent(t, copies, sem):
        wait_for(inc_all.at[t, pl.ds(0, blocks), pl.ds(0, copies)], sem)

    for t in range(ticks):
        wait_for(x_all.at[t, pl.ds(0, blocks), pl.ds(0, places)], x_send.at[t])
        wait_for(x_all.at[t, pl.ds(0, blocks), pl.ds(0, places)], xf_send.at[t])
        sent(t, len(FAR_FIRST) if t == 0 else len(NEAR), ag_send.at[t])
        sent(t, places, agf_send.at[t])
        wait_for(core_in.at[t], core_send.at[t])
        wait_for(rs_in.at[t], rs_send.at[t])
    for t in range(ticks - 1):
        @pl.when(section > 0)
        def _():
            sent(t, 1 + len(FLIPPED), up_send.at[t])

        @pl.when(section == sections - 1)
        def _():
            sent(t, len(FLIPPED), top_send.at[t])


def solution(mesh):
    sections, tps = mesh.shape["section"], mesh.shape["tp"]

    def body(stash, w_in, w_out, gain, plan, arriving, fresh):
        stash, w_in, w_out, arriving = stash[0], w_in[0], w_out[0], arriving[0]
        stash, fresh = jnp.swapaxes(stash, 0, 1), jnp.swapaxes(fresh, 0, 1)
        rows, slots, width = stash.shape
        ticks = plan.shape[0]
        units = w_out.shape[0]
        places = tps // 2
        blocks = width // BLOCK
        vmem = pl.BlockSpec(memory_space=pltpu.VMEM)
        hbm = pl.BlockSpec(memory_space=pl.ANY)
        each = pltpu.SemaphoreType.DMA((ticks,))
        each_block = pltpu.SemaphoreType.DMA((ticks, blocks))
        results = pl.pallas_call(
            functools.partial(window_kernel, sections, tps, ticks),
            out_shape=pltpu.VMEM((ticks, rows, width), bf16),
            in_specs=[hbm] * 7,
            out_specs=vmem,
            scratch_shapes=[
                pltpu.SMEM(plan.shape, plan.dtype),
                pltpu.VMEM(stash.shape, bf16),
                pltpu.VMEM(gain.shape, f32),
                pltpu.VMEM(arriving.shape, bf16),
                pltpu.VMEM(fresh.shape, bf16),
                pltpu.VMEM((width, units), bf16),
                pltpu.VMEM((units, width), bf16),
                pltpu.VMEM((ticks, blocks, SUB, WIRE), bf16),
                pltpu.VMEM((ticks, blocks, tps, SUB, WIRE), bf16),
                pltpu.VMEM((ticks, blocks, tps, SUB, WIRE), bf16),
                pltpu.VMEM((tps * PAD, units), f32),
                pltpu.VMEM((tps * PAD, units), f32),
                pltpu.VMEM((tps * PAD, units), bf16),
                pltpu.VMEM((blocks, tps * PAD, BLOCK), f32),
                pltpu.VMEM((blocks, tps, SUB, WIRE), f32),
                pltpu.VMEM((ticks, blocks, tps, SUB, WIRE), bf16),
                pltpu.VMEM((ticks, blocks, places, SUB, WIRE), bf16),
                pltpu.VMEM((ticks, blocks, places, SUB, WIRE), bf16),
                pltpu.VMEM((ticks, blocks, places - 1, SUB, WIRE), bf16),
                pltpu.VMEM((ticks, blocks, SUB, WIRE), bf16),
                pltpu.VMEM((PAD, width), f32),
                pltpu.SemaphoreType.DMA((7,)),
                each, each_block, each, each_block,
                each, each_block, each, each_block,
                each, each_block, each, each_block,
                each, each_block, each,
            ],
            compiler_params=pltpu.CompilerParams(
                collective_id=0, has_side_effects=True, vmem_limit_bytes=60 * 2**20),
            name="window",
        )(plan, stash, w_in, w_out, gain, arriving, fresh)
        return results[:, None]

    placed = (
        P("section", None, "tp", None),
        P("section", None, "tp"),
        P("section", "tp", None),
        P("section", None),
        P(),
        P("section", "tp", None),
        P(None, "tp", None),
    )
    return jax.shard_map(
        body, mesh=mesh, in_specs=placed, out_specs=P(None, "section", "tp", None), check_vma=False
    )
```

```python
import functools

import jax
import jax.numpy as jnp
from jax import lax
from jax.experimental import pallas as pl
from jax.experimental.pallas import tpu as pltpu
from jax.sharding import PartitionSpec as P

epsilon = 1e-06
contract_last = (((1,), (1,)), ((), ()))
bf16, f32 = jnp.bfloat16, jnp.float32
PAD = 16
IN_TILE = 1024
BLOCK = 256
LANES = 128
SUB = 8
WIRE = BLOCK + LANES
FAR_FIRST = (5, 7, 1, 3, 4, 6, 2)
FLIPPED = (5, 7, 3)
NEAR = (1, 4, 6, 2)
AHEAD = 3


def packed(value):
    low = value[:, SUB:, :LANES]
    high = pltpu.roll(value[:, SUB:, LANES:], 4, 1)
    row = lax.broadcasted_iota(jnp.int32, low.shape, 1)
    return jnp.concatenate([value[:, :SUB], jnp.where(row < 4, low, high)], axis=2)


def unpacked(wire):
    wire = wire.astype(f32)
    tail = wire[:, :, BLOCK:]
    bottom = jnp.concatenate([tail, pltpu.roll(tail, 4, 1)], axis=2)
    return jnp.concatenate([wire[:, :, :BLOCK], bottom], axis=1)


def window_kernel(
    sections, tps, ticks,
    plan_in, stash_in, w_in, w_out, gain_in, arriving_in, fresh_in, out,
    plan, stash, gain, arriving, fresh, wi, wo, picks, x_all, inc_all, factor, back_sum, hidden, raw, acc, part, core_in, half, rs_in, out_v, pad_v,
    load_sem, x_send, x_recv, xf_send, xf_recv, ag_send, ag_recv, agf_send, agf_recv,
    core_send, core_recv, rs_send, rs_recv, up_send, up_recv, top_send,
):
    section = lax.axis_index("section")
    me = lax.axis_index("tp")
    core = lax.rem(me, 2)
    place = me // 2
    places = tps // 2
    rows, slots, width = stash.shape
    units = wo.shape[0]
    blocks = width // BLOCK
    mirror = lax.rem(section + sections // 2, sections)
    above = lax.rem(section + 1, sections)
    below = lax.rem(section + sections - 1, sections)
    mine = pl.multiple_of(core * places, places)
    theirs = pl.multiple_of((1 - core) * places, places)
    own = mine + place
    partner = me + 1 - 2 * core

    def remote(src, dst, send, recv, to_section, to_tp):
        return pltpu.make_async_remote_copy(
            src_ref=src, dst_ref=dst, send_sem=send, recv_sem=recv,
            device_id={"section": to_section, "tp": to_tp}, device_id_type=pl.DeviceIdType.MESH)

    def wait_for(ref, sem):
        pltpu.make_async_copy(ref, ref, sem).wait()

    def at_place(k):
        return lax.bitwise_xor(place, k) * 2 + core

    def cols_of(b):
        return slice(b * BLOCK, (b + 1) * BLOCK)

    barrier = pltpu.get_barrier_semaphore()

    def greet(to_section, to_tp):
        pl.semaphore_signal(barrier, inc=1, device_id={"section": to_section, "tp": to_tp},
                            device_id_type=pl.DeviceIdType.MESH)

    for k in FAR_FIRST:
        greet(section, at_place(k))
    for k in FAR_FIRST + (0,):
        greet(mirror, at_place(k))
    for k in FLIPPED + (0,):
        greet(above, at_place(k))
        greet(below, at_place(k))
    greet(section, partner)

    pairs = ((plan_in, plan), (stash_in, stash), (arriving_in, arriving), (gain_in, gain), (fresh_in, fresh), (w_in, wi), (w_out, wo))
    loads = [pltpu.make_async_copy(src, dst, load_sem.at[n]) for n, (src, dst) in enumerate(pairs)]
    for load in loads[:-1]:
        load.start()
    pad_v[...] = jnp.zeros_like(pad_v)
    for load in loads[:3]:
        load.wait()

    def wire_blocks(value):
        pad_v[0:rows] = value.astype(f32)
        return [packed(pad_v[:, cols_of(b)][None])[0].astype(bf16) for b in range(blocks)]

    def set_own(t, value):
        for b, block in enumerate(wire_blocks(value)):
            inc_all[t, b, own] = block

    def set_pick(t):
        slot = plan[t, mirror]
        pick = stash[:, 0, :]
        for k in range(1, slots):
            pick = jnp.where(slot == k, stash[:, k, :], pick)
        for b, block in enumerate(wire_blocks(pick)):
            picks[t, b] = block

    set_pick(0)
    set_own(0, arriving[...])
    pl.semaphore_wait(barrier, 2 * places + 2 * (1 + len(FLIPPED)))

    def send_x(t, parts):
        for b in parts:
            for k in FAR_FIRST + (0,):
                remote(picks.at[t, b], x_all.at[t, b, own], x_send.at[t], x_recv.at[t, b],
                       mirror, at_place(k)).start()

    def send_x_whole(t):
        for k in FAR_FIRST + (0,):
            remote(picks.at[t], x_all.at[t, pl.ds(0, blocks), own], x_send.at[t], x_recv.at[t, 0],
                   mirror, at_place(k)).start()

    def forward_x_whole(t):
        block = x_all.at[t, pl.ds(0, blocks), pl.ds(mine, places)]
        wait_for(block, x_recv.at[t, 0])
        remote(block, block, xf_send.at[t], xf_recv.at[t, 0], section, partner).start()

    def send_own(t, b, to_places, send):
        for k in to_places:
            remote(inc_all.at[t, b, own], inc_all.at[t, b, own], send, ag_recv.at[t, b],
                   section, at_place(k)).start()

    def forward_x(t, b):
        block = x_all.at[t, b, pl.ds(mine, places)]
        wait_for(block, x_recv.at[t, b])
        remote(block, block, xf_send.at[t], xf_recv.at[t, b], section, partner).start()

    def forward_incoming(t, b):
        wait_for(inc_all.at[t, b, pl.ds(0, places - 1)], ag_recv.at[t, b])
        block = inc_all.at[t, b, pl.ds(mine, places)]
        remote(block, block, agf_send.at[t], agf_recv.at[t, b], section, partner).start()

    def preact(t, b, scale_in, scale_out):
        values = unpacked(x_all[t, b]).reshape(tps * PAD, BLOCK)
        if scale_in is not None:
            values = values * scale_in
        inputs = (values * gain[:, cols_of(b)]).astype(bf16)
        for n in range(units // IN_TILE):
            cols = slice(n * IN_TILE, (n + 1) * IN_TILE)
            pre = jnp.dot(inputs, wi[cols_of(b), cols], preferred_element_type=f32)
            if b > 0:
                pre = pre + factor[:, cols]
            if b == blocks - 1:
                pre = scale_out * jnp.maximum(pre, 0.0)
            factor[:, cols] = pre

    def x_square(t, b):
        wait_for(x_all.at[t, b, pl.ds(theirs, places)], xf_recv.at[t, b])
        return row_square(t, b)

    def row_square(t, b):
        values = unpacked(x_all[t, b]).reshape(tps * PAD, BLOCK)
        return jnp.sum(values * values, axis=-1, keepdims=True)

    def rms_of(square):
        return lax.rsqrt(square * (1.0 / width) + epsilon)

    def first_matmul(t, b):
        wait_for(inc_all.at[t, b, pl.ds(theirs, places)], agf_recv.at[t, b])
        incoming = unpacked(inc_all[t, b]).reshape(tps * PAD, BLOCK).astype(bf16)
        for n in range(units // IN_TILE):
            cols = slice(n * IN_TILE, (n + 1) * IN_TILE)
            back = lax.dot_general(incoming, wo[cols, cols_of(b)], contract_last, preferred_element_type=f32)
            if b > 0:
                back = back + back_sum[:, cols]
            if b == blocks - 1:
                hidden[:, cols] = (back * factor[:, cols]).astype(bf16)
            else:
                back_sum[:, cols] = back

    def second_matmul(b):
        raw[b] = lax.dot_general(hidden[...], wi[cols_of(b), :], contract_last, preferred_element_type=f32)

    def pack_part(t, b):
        total = packed(raw[b].reshape(tps, PAD, BLOCK))
        acc[b] = total
        part[t, b] = total.astype(bf16)

    def send_part(t, b):
        remote(part.at[t, b, pl.ds(theirs, places)], core_in.at[t, b], core_send.at[t], core_recv.at[t, b],
               section, partner).start()

    def take_part(t, b):
        wait_for(core_in.at[t, b], core_recv.at[t, b])

    def pack_half(t, b):
        half[t, b] = (acc[b, pl.ds(mine, places)] + core_in[t, b].astype(f32)).astype(bf16)

    def scatter(t, b):
        for k in FAR_FIRST:
            remote(half.at[t, b, lax.bitwise_xor(place, k)], rs_in.at[t, b, k - 1], rs_send.at[t], rs_recv.at[t, b],
                   section, at_place(k)).start()

    send_x(0, range(blocks))
    for b in range(blocks):
        send_own(0, b, FAR_FIRST, ag_send.at[0])
    loads[6].start()
    for t in range(1, ticks):
        set_pick(t)
    loads[3].wait()
    loads[4].wait()

    @pl.when(section == sections - 1)
    def _():
        for t in range(1, ticks):
            set_own(t, fresh[:, t - 1, :])

    for b in range(AHEAD):
        forward_x(0, b)
    loads[5].wait()
    for b in range(blocks):
        square = x_square(0, b) if b == 0 else square + x_square(0, b)
        preact(0, b, None, 2.0 * rms_of(square) if b == blocks - 1 else None)
        if b + AHEAD < blocks:
            forward_x(0, b + AHEAD)
        else:
            forward_incoming(0, b + AHEAD - blocks)
    loads[6].wait()

    def tick(t, carry):
        more = t + 1 < ticks
        for b in range(blocks):
            first_matmul(t, b)
            if b + AHEAD < blocks:
                forward_incoming(t, b + AHEAD)
            if b == 0:
                @pl.when(more)
                def _():
                    send_x_whole(t + 1)
        second_matmul(0)
        for b in range(1, blocks):
            second_matmul(b)
            pack_part(t, b - 1)
            if b > 2:
                pack_half(t, b - 3)
            send_part(t, b - 1)
            if b > 2:
                scatter(t, b - 3)
            if b > 1 and b < blocks - 1:
                take_part(t, b - 2)
        pack_part(t, blocks - 1)
        send_part(t, blocks - 1)
        for b in range(blocks - 3, blocks):
            take_part(t, b)
            pack_half(t, b)
            scatter(t, b)
        values = jnp.concatenate([unpacked(x_all[t, b, pl.ds(own, 1)])[0] for b in range(blocks)], axis=1)
        inverse_rms = lax.rsqrt(jnp.mean(values * values, axis=-1, keepdims=True) + epsilon)
        normed = values * inverse_rms
        incoming = jnp.concatenate([unpacked(inc_all[t, b, pl.ds(own, 1)])[0] for b in range(blocks)], axis=1)
        scaled = []
        for b in range(blocks):
            wait_for(rs_in.at[t, b], rs_recv.at[t, b])
            total = (acc[b, pl.ds(own, 1)] + core_in[t, b, pl.ds(place, 1)].astype(f32)
                     + jnp.sum(rs_in[t, b].astype(f32), axis=0, keepdims=True))
            scaled.append(unpacked(total)[0] * gain[:, cols_of(b)])
        scaled = jnp.concatenate(scaled, axis=1)
        inner = jnp.mean(scaled * normed, axis=-1, keepdims=True)
        result = incoming + inverse_rms * (scaled - normed * inner)
        for b in range(blocks):
            out_v[t, b] = packed(result[:, cols_of(b)][None])[0].astype(bf16)

        @pl.when(jnp.logical_and(more, section > 0))
        def _():
            for b in range(blocks):
                remote(out_v.at[t, b], inc_all.at[t + 1, b, own], up_send.at[t], up_recv.at[t, b], below, me).start()
            for b in range(blocks):
                for k in FLIPPED:
                    remote(out_v.at[t, b], inc_all.at[t + 1, b, own], up_send.at[t], ag_recv.at[t + 1, b],
                           below, at_place(k)).start()

        @pl.when(jnp.logical_and(more, section == sections - 1))
        def _():
            for b in range(blocks):
                send_own(t + 1, b, FLIPPED, top_send.at[t])

        out[t] = result[0:rows].astype(bf16)

        @pl.when(more)
        def _():
            forward_x_whole(t + 1)
            for b in range(blocks):
                @pl.when(section < sections - 1)
                def _():
                    wait_for(inc_all.at[t + 1, b, own], up_recv.at[t, b])

                send_own(t + 1, b, NEAR, ag_send.at[t + 1])

            wait_for(x_all.at[t + 1, pl.ds(0, blocks), pl.ds(theirs, places)], xf_recv.at[t + 1, 0])
            square = row_square(t + 1, 0)
            for b in range(1, blocks):
                square = square + row_square(t + 1, b)
            for b in range(blocks):
                preact(t + 1, b, rms_of(square), 2.0)
            for b in range(AHEAD):
                forward_incoming(t + 1, b)

        return carry

    lax.fori_loop(0, ticks, tick, 0)

    def sent(t, copies, sem):
        wait_for(inc_all.at[t, pl.ds(0, blocks), pl.ds(0, copies)], sem)

    for t in range(ticks):
        wait_for(x_all.at[t, pl.ds(0, blocks), pl.ds(0, places)], x_send.at[t])
        wait_for(x_all.at[t, pl.ds(0, blocks), pl.ds(0, places)], xf_send.at[t])
        sent(t, len(FAR_FIRST) if t == 0 else len(NEAR), ag_send.at[t])
        sent(t, places, agf_send.at[t])
        wait_for(core_in.at[t], core_send.at[t])
        wait_for(rs_in.at[t], rs_send.at[t])
    for t in range(ticks - 1):
        @pl.when(section > 0)
        def _():
            sent(t, 1 + len(FLIPPED), up_send.at[t])

        @pl.when(section == sections - 1)
        def _():
            sent(t, len(FLIPPED), top_send.at[t])


def solution(mesh):
    sections, tps = mesh.shape["section"], mesh.shape["tp"]

    def body(stash, w_in, w_out, gain, plan, arriving, fresh):
        stash, w_in, w_out, arriving = stash[0], w_in[0], w_out[0], arriving[0]
        stash, fresh = jnp.swapaxes(stash, 0, 1), jnp.swapaxes(fresh, 0, 1)
        rows, slots, width = stash.shape
        ticks = plan.shape[0]
        units = w_out.shape[0]
        places = tps // 2
        blocks = width // BLOCK
        vmem = pl.BlockSpec(memory_space=pltpu.VMEM)
        hbm = pl.BlockSpec(memory_space=pl.ANY)
        each = pltpu.SemaphoreType.DMA((ticks,))
        each_block = pltpu.SemaphoreType.DMA((ticks, blocks))
        results = pl.pallas_call(
            functools.partial(window_kernel, sections, tps, ticks),
            out_shape=pltpu.VMEM((ticks, rows, width), bf16),
            in_specs=[hbm] * 7,
            out_specs=vmem,
            scratch_shapes=[
                pltpu.SMEM(plan.shape, plan.dtype),
                pltpu.VMEM(stash.shape, bf16),
                pltpu.VMEM(gain.shape, f32),
                pltpu.VMEM(arriving.shape, bf16),
                pltpu.VMEM(fresh.shape, bf16),
                pltpu.VMEM((width, units), bf16),
                pltpu.VMEM((units, width), bf16),
                pltpu.VMEM((ticks, blocks, SUB, WIRE), bf16),
                pltpu.VMEM((ticks, blocks, tps, SUB, WIRE), bf16),
                pltpu.VMEM((ticks, blocks, tps, SUB, WIRE), bf16),
                pltpu.VMEM((tps * PAD, units), f32),
                pltpu.VMEM((tps * PAD, units), f32),
                pltpu.VMEM((tps * PAD, units), bf16),
                pltpu.VMEM((blocks, tps * PAD, BLOCK), f32),
                pltpu.VMEM((blocks, tps, SUB, WIRE), f32),
                pltpu.VMEM((ticks, blocks, tps, SUB, WIRE), bf16),
                pltpu.VMEM((ticks, blocks, places, SUB, WIRE), bf16),
                pltpu.VMEM((ticks, blocks, places, SUB, WIRE), bf16),
                pltpu.VMEM((ticks, blocks, places - 1, SUB, WIRE), bf16),
                pltpu.VMEM((ticks, blocks, SUB, WIRE), bf16),
                pltpu.VMEM((PAD, width), f32),
                pltpu.SemaphoreType.DMA((7,)),
                each, each_block, each, each_block,
                each, each_block, each, each_block,
                each, each_block, each, each_block,
                each, each_block, each,
            ],
            compiler_params=pltpu.CompilerParams(
                collective_id=0, has_side_effects=True, vmem_limit_bytes=60 * 2**20),
            name="window",
        )(plan, stash, w_in, w_out, gain, arriving, fresh)
        return results[:, None]

    placed = (
        P("section", None, "tp", None),
        P("section", None, "tp"),
        P("section", "tp", None),
        P("section", None),
        P(),
        P("section", "tp", None),
        P(None, "tp", None),
    )
    return jax.shard_map(
        body, mesh=mesh, in_specs=placed, out_specs=P(None, "section", "tp", None), check_vma=False
    )
```
